32 devices in a mesh: section: 2 (over x), expert: 16 (over z, y, core).
Axes of the slice: x: 2, y: 2, z: 4, core: 2. Of those that a mesh axis runs over, the one named last changes fastest.
Arguments:
- tokens: bfloat16 [2, 256, 2048], P('section', 'expert'), may hold values from -6 to 6
- out_grad: bfloat16 [2, 256, 2048], P('section', 'expert'), may hold values from -1 to 1
- expert_ids: int32 [2, 256, 2], P('section'), may hold values from 0 to 3, all different within a row; in each aligned block of 16 rows (0 to 15, 16 to 31, ..., all dimensions but the last counted through in order) at most 14 rows name the same one
- gate_weights: bfloat16 [2, 256, 2], P('section'), may hold values from 0.049804688 to 1
- gate_up_rows: bfloat16 [2, 16, 384, 2048], P('section', 'expert'), may hold values from -0.125 to 0.125
- down_rows: bfloat16 [2, 16, 192, 2048], P('section', 'expert'), may hold values from -0.21875 to 0.21875
Outputs:
- gate_grad: float32 [2, 256, 2], P('section', 'expert')
- handed: bfloat16 [2, 256, 2048], P('section', 'expert')
The draws below stay inside these ranges and needn't reach their ends.
Inputs may be any that keep to these rules, and one draw needn't show every extreme that they name: `expert_ids`: within the rows of one device (16 consecutive rows of a section), every expert id appears in at most 14 rows, and some id reaches 14; the 2 ids of a row are distinct.
All inputs are finite; a program needn't handle non-finite values.
Results may differ from the reference program's by a relative error of at most 0.0049.
Values may be sent and summed in bfloat16 or wider, within the bound.
No kernel may reach another device: no remote copies, remote signals or barrier semaphores. Data moves between devices by JAX's collectives and lax.ppermute only.
A program may use at most 64 MiB of HBM per device.

```python
import math
import jax
import jax.numpy as jnp
import numpy as np
from jax import lax

D = 2048
FF = 768
TOK_DEV = 16
TOPK = 2
EXPERTS = 4
SPLIT = 4
FF_PART = 192
MOST = 14
TOKENS = 256
N_SECTION = 2
N_EXPERT = 16


def steps_of(own_key, dims, cuts, least, top_value):
    gain = 1.0
    for position, parts in cuts:
        heights = jax.random.uniform(jax.random.fold_in(jax.random.fold_in(own_key, 6), position), (parts,), jnp.float32, least / len(cuts), top_value / len(cuts))
        gain = gain * jnp.repeat(jnp.exp(heights), dims[position] // parts).reshape((-1,) + (1,) * (len(dims) - 1 - position))
    return gain


def assign_block(key, own, number, rows, count, top, bound, slope):
    order = jax.random.permutation(key, count)
    crowded, ordinary = load_shares(count, rows * top, bound, slope, True), load_shares(count, rows * top, bound, slope, False)
    places = jnp.arange(count)

    def named(sizes, rotation):
        used = int((sizes > 0).sum())
        fixed = max(1, used // 4)
        moved = fixed + (places - fixed + rotation * (used - fixed)) % max(1, count - fixed)
        return jnp.zeros((count,), jnp.int32).at[order[jnp.where(places < fixed, places, moved)]].set(jnp.asarray(sizes, jnp.int32))

    sizes = jnp.where(number % 4 == 0, named(crowded, number // 4), named(ordinary, number - number // 4 - 1))
    mixed = jax.random.permutation(jax.random.fold_in(own, 3), count)
    donor, sink = mixed[0:count // 2 * 2:2], mixed[1:count // 2 * 2:2]
    room = jnp.minimum(sizes[donor] - 1, bound - sizes[sink]) // 2
    room = jnp.where((donor == order[0]) | (sink == order[0]) | (sizes[sink] == 0), 0, jnp.maximum(room, 0))
    moved = jax.random.randint(jax.random.fold_in(own, 4), (count // 2,), 0, 1 << 20) % (room + 1)
    sizes = sizes.at[donor].add(-moved).at[sink].add(moved)
    items = jnp.searchsorted(jnp.cumsum(sizes), jnp.arange(rows * top), side="right").astype(jnp.int32)
    table = items.reshape(top, rows).T
    table = table[jax.random.permutation(jax.random.fold_in(own, 1), rows)]
    rotation = jax.random.randint(jax.random.fold_in(own, 2), (rows, 1), 0, top)
    return jnp.take_along_axis(table, (jnp.arange(top)[None, :] + rotation) % top, axis=1)


def load_shares(amount, total, reach, skew, full):
    loads = [(1 << 20) // math.isqrt(standing ** skew) + 1 for standing in range(1, amount + 1)]
    largest = reach if full else min(reach, max(-(-total // amount), total * loads[0] // sum(loads)))
    least = 1 if total - largest >= amount - 1 else 0
    counts, rest = [largest] + [least] * (amount - 1), total - largest - least * (amount - 1)
    while rest > 0:
        candidates = [i for i in range(1, amount) if counts[i] < largest] or [i for i in range(1, amount) if counts[i] < reach]
        pool, left = sum([loads[i] for i in candidates]), rest
        for i in candidates:
            extra = min(reach - counts[i], max(1, left * loads[i] // pool), rest)
            counts[i] = counts[i] + extra
            rest = rest - extra
    return np.array(counts)


def scatter_about(own_key, shape, deviation, most, shards=(), kind=jnp.bfloat16):
    loudness = steps_of(own_key, shape, shards, -0.22, 0.18) if shards else 1.0
    drawn = jax.random.normal(own_key, shape, jnp.float32) * deviation * loudness
    return jnp.minimum(jnp.maximum(drawn, -most), most).astype(kind)


def setup_inputs(seed: int = 0) -> dict:
    keys = jax.random.split(jax.random.key(seed), 7)
    tokens = scatter_about(keys[0], (N_SECTION, TOKENS, D), 1.0, 6.0, ((0, 2), (1, 16)))
    out_grad = scatter_about(keys[1], (N_SECTION, TOKENS, D), 0.15, 1.0, ((0, 2), (1, 16)))
    expert_ids_keys = jax.random.split(jax.random.fold_in(keys[2], 1), N_SECTION * TOKENS // TOK_DEV)
    expert_ids_turns = jax.random.permutation(jax.random.fold_in(keys[2], 3), N_SECTION * TOKENS // TOK_DEV)
    expert_ids = jax.vmap(lambda own, number: assign_block(jax.random.fold_in(keys[2], 2), own, number, TOK_DEV, EXPERTS, TOPK, MOST, 2))(expert_ids_keys, expert_ids_turns).reshape((N_SECTION, TOKENS, TOPK))
    gate_weights = jnp.clip(jnp.exp(math.log(1.0) - 2.9996462 * jax.random.uniform(keys[3], (N_SECTION, TOKENS, TOPK), jnp.float32) ** steps_of(keys[3], (N_SECTION, TOKENS, TOPK), ((0, 2),), -0.2, 0.2)), 0.049804688, 1.0).astype(jnp.bfloat16)
    gate_up_rows = scatter_about(keys[4], (N_SECTION, N_EXPERT, 2 * FF_PART, D), D ** -0.5, 0.125, ((0, 2), (1, 16)))
    down_rows = scatter_about(keys[5], (N_SECTION, N_EXPERT, FF_PART, D), FF ** -0.5, 0.21875, ((0, 2), (1, 16)))
    return dict(tokens=tokens, out_grad=out_grad, expert_ids=expert_ids, gate_weights=gate_weights, gate_up_rows=gate_up_rows, down_rows=down_rows)


def slot_table(matches, capacity):
    ranked = jnp.cumsum(matches, axis=-1) - 1.0
    levels = jnp.arange(capacity, dtype=jnp.float32)
    return matches[..., None, :] * (ranked[..., None, :] == levels[:, None]).astype(jnp.float32)


def expert_grads(rows_in, rows_grad, slot_gate, gate_up, down_mat):
    width = down_mat.shape[0]
    both = jnp.dot(rows_in, gate_up.T, preferred_element_type=jnp.float32)
    first = both[:, :width]
    second = both[:, width:]
    back = jnp.dot(rows_grad, down_mat.T, preferred_element_type=jnp.float32)
    sigma = jax.nn.sigmoid(first)
    active = first * sigma
    slot_grad = jnp.sum(back * active * second, axis=1)
    scaled = slot_gate[:, None] * back
    d_first = scaled * second * sigma * (1.0 + first * (1.0 - sigma))
    d_second = scaled * active
    d_both = jnp.concatenate([d_first, d_second], axis=1).astype(jnp.bfloat16)
    contrib = jnp.dot(d_both, gate_up, preferred_element_type=jnp.float32)
    return contrib, slot_grad


def section_grads(packed):
    tokens, out_grad, expert_ids, gate_weights, gate_up_rows, down_rows = packed
    blocks = N_EXPERT
    pairs = TOK_DEV * TOPK
    gates = gate_weights.astype(jnp.float32).reshape(blocks, 1, pairs)
    block_in = tokens.reshape(blocks, TOK_DEV, D).astype(jnp.float32)
    block_grad = out_grad.reshape(blocks, TOK_DEV, D).astype(jnp.float32)
    total = jnp.zeros((blocks, TOK_DEV, D), jnp.float32)
    gate_total = jnp.zeros((blocks, pairs), jnp.float32)
    for expert_no in range(EXPERTS):
        matches = (expert_ids.reshape(blocks, pairs) == expert_no).astype(jnp.float32)
        slot_pick = slot_table(matches, MOST)
        chooser = slot_pick.reshape(blocks, MOST, TOK_DEV, TOPK).sum(axis=-1)
        slot_gate = jnp.sum(slot_pick * gates, axis=-1).reshape(-1)
        rows_in = jnp.einsum("jrt,jtd->jrd", chooser, block_in).astype(jnp.bfloat16).reshape(-1, D)
        rows_grad = jnp.einsum("jrt,jtd->jrd", chooser, block_grad).astype(jnp.bfloat16).reshape(-1, D)
        lower = expert_no * SPLIT
        gate_mat = gate_up_rows[lower:lower + SPLIT, :FF_PART, :].reshape(FF, D)
        up_mat = gate_up_rows[lower:lower + SPLIT, FF_PART:, :].reshape(FF, D)
        down_mat = down_rows[lower:lower + SPLIT].reshape(FF, D)
        gate_up = jnp.concatenate([gate_mat, up_mat], axis=0)
        contrib, slot_grad = expert_grads(rows_in, rows_grad, slot_gate, gate_up, down_mat)
        total = total + jnp.einsum("jrt,jrd->jtd", chooser, contrib.reshape(blocks, MOST, D).astype(jnp.float32))
        gate_total = gate_total + jnp.einsum("jrp,jr->jp", slot_pick, slot_grad.reshape(blocks, MOST).astype(jnp.float32))
    return total.reshape(TOKENS, D).astype(jnp.bfloat16), gate_total.reshape(TOKENS, TOPK)


def reference(tokens, out_grad, expert_ids, gate_weights, gate_up_rows, down_rows):
    input_grad, gate_grad = lax.map(section_grads, (tokens, out_grad, expert_ids, gate_weights, gate_up_rows, down_rows))
    handed = jnp.concatenate([input_grad[1:], jnp.zeros_like(input_grad[:1])], axis=0)
    return gate_grad, handed
```

```python
import functools

import jax
import jax.numpy as jnp
from jax import lax
from jax.experimental import pallas as pl
from jax.experimental.pallas import tpu as pltpu
from jax.sharding import PartitionSpec as P

PAD = 128


def locate(position):
    return position // 4, position // 2 % 2, position % 2


def fetch(value, dz, dy, dc):
    size = lax.axis_size("expert")
    pairs = []
    for target in range(size):
        z, y, c = locate(target)
        source = (z + dz) % (size // 4) * 4 + (y ^ dy) * 2 + (c ^ dc)
        pairs.append((source, target))
    return lax.ppermute(value, "expert", pairs)


def from_behind(shard, axis, by):
    length = lax.axis_size(axis)
    pairs = [(i, i + by) for i in range(length) if 0 <= i + by < length]
    return lax.ppermute(shard, axis, pairs)


def split_columns(gates):
    high = gates.astype(jnp.bfloat16)
    low = (gates - high.astype(jnp.float32)).astype(jnp.bfloat16)
    return high, low


def grads_kernel(count, *refs):
    blocks, (aux_ref, gate_up_ref, down_ref, out_ref) = refs[:count], refs[count:]
    width = down_ref.shape[0]
    model = gate_up_ref.shape[1]
    rows_in = jnp.concatenate([ref[0] for ref in blocks], axis=0)
    rows_grad = jnp.concatenate([ref[1] for ref in blocks], axis=0)
    contract = (((1,), (1,)), ((), ()))
    both = lax.dot_general(rows_in, gate_up_ref[...], contract, preferred_element_type=jnp.float32)
    back = lax.dot_general(rows_grad, down_ref[...], contract, preferred_element_type=jnp.float32)
    first = both[:, :width]
    second = both[:, width:]
    sigma = jax.nn.sigmoid(first)
    active = first * sigma
    aux = aux_ref[...]
    gate = aux[:, 0:1]
    slot_grad = jnp.sum(back * active * second, axis=1, keepdims=True)
    scaled = gate * back
    d_first = scaled * second * sigma * (1.0 + first * (1.0 - sigma))
    d_second = scaled * active
    d_both = jnp.concatenate([d_first, d_second], axis=1).astype(jnp.bfloat16)
    contrib = jnp.dot(d_both, gate_up_ref[...], preferred_element_type=jnp.float32)
    out_ref[:, :model] = contrib.astype(jnp.bfloat16)
    lane = lax.broadcasted_iota(jnp.int32, (aux.shape[0], PAD), 1)
    picked = jnp.where(lane % 2 == 0, aux[:, 1:2], aux[:, 2:3]) * slot_grad
    high = picked.astype(jnp.bfloat16).astype(jnp.float32)
    low = picked - high
    packed = jnp.where(lane < 2, high, jnp.where(lane < 4, low, 0.0))
    out_ref[:, model:] = packed.astype(jnp.bfloat16)


def expert_grads(blocks, aux, gate_up, down_mat):
    rows = aux.shape[0]
    model = gate_up.shape[1]
    return pl.pallas_call(
        functools.partial(grads_kernel, len(blocks)),
        out_shape=jax.ShapeDtypeStruct((rows, model + PAD), jnp.bfloat16),
        compiler_params=pltpu.CompilerParams(vmem_limit_bytes=40 << 20),
    )(*blocks, aux, gate_up, down_mat)


def unpack(block, model):
    wide = block.astype(jnp.float32)
    return wide[:, :model], wide[:, model:]


def pair_kernel(near_ref, far_ref, out_ref):
    model = out_ref.shape[1] - PAD
    total = near_ref[:, :model].astype(jnp.float32) + far_ref[:, :model].astype(jnp.float32)
    out_ref[:, :model] = total.astype(jnp.bfloat16)
    gates = near_ref[:, model:].astype(jnp.float32) + far_ref[:, model:].astype(jnp.float32)
    lane = lax.broadcasted_iota(jnp.int32, gates.shape, 1)
    shifted = pltpu.roll(gates, PAD - 2, 1)
    value = gates + shifted
    high = value.astype(jnp.bfloat16).astype(jnp.float32)
    low = pltpu.roll(value - high, 2, 1)
    packed = jnp.where(lane < 2, high, jnp.where(lane < 4, low, 0.0))
    out_ref[:, model:] = packed.astype(jnp.bfloat16)


def last_kernel(count, *refs):
    parts, (rows_ref, gates_ref) = refs[:count], refs[count:]
    model = rows_ref.shape[1]
    total = parts[0][:, :model].astype(jnp.float32)
    gates = parts[0][:, model:].astype(jnp.float32)
    for ref in parts[1:]:
        total = total + ref[:, :model].astype(jnp.float32)
        gates = gates + ref[:, model:].astype(jnp.float32)
    rows_ref[...] = total.astype(jnp.bfloat16)
    gates_ref[...] = gates + pltpu.roll(gates, PAD - 2, 1)


def body(tokens, out_grad, expert_ids, gate_weights, gate_up_rows, down_rows):
    size = lax.axis_size("expert")
    planes = size // 4
    expert_count = max(2, size // 4)
    part_count = size // expert_count
    position = lax.axis_index("expert")
    my_expert = position // part_count
    block_rows = tokens.shape[1]
    model = tokens.shape[2]
    routes = expert_ids.shape[2]
    gate_up = gate_up_rows[0, 0]
    down_mat = down_rows[0, 0]

    own = jnp.concatenate([tokens, out_grad], axis=0)
    across = [fetch(own, dz, 0, 0) for dz in range(1, planes)]
    line = [own] + across
    other = [fetch(value, 0, 1, 0) for value in line]
    near = [value for pair in zip(line, other) for value in pair]
    far = [fetch(value, 0, 0, 1) for value in near]

    half = size // 2
    z, y, c = locate(position)
    order = jnp.arange(size)
    oc, oz, oy = order // half, order % half // 2, order % 2
    source = (z + oz) % planes * 4 + (y ^ oy) * 2 + (c ^ oc)
    ids = expert_ids[0].reshape(size, block_rows, routes)[source].reshape(-1, routes)
    gates = gate_weights[0].astype(jnp.float32).reshape(size, block_rows, routes)[source].reshape(-1, routes)
    match = (ids == my_expert).astype(jnp.float32)
    gate = jnp.sum(match * gates, axis=1, keepdims=True)
    aux = jnp.concatenate([gate, match, jnp.zeros((gate.shape[0], PAD - 1 - routes), jnp.float32)], axis=1)

    rows = half * block_rows
    send = expert_grads(far, aux[rows:], gate_up, down_mat)
    keep = expert_grads(near, aux[:rows], gate_up, down_mat)
    received = fetch(send, 0, 0, 1)
    width = model + PAD
    paired = pl.pallas_call(
        pair_kernel,
        out_shape=jax.ShapeDtypeStruct((rows, width), jnp.bfloat16),
    )(keep, received).reshape(planes, 2, block_rows, width)
    parts = [paired[0, 0]]
    for dz in range(planes):
        for dy in range(2):
            if dz or dy:
                parts.append(fetch(paired[dz, dy], -dz, dy, 0))
    grad_rows, gate_lanes = pl.pallas_call(
        functools.partial(last_kernel, len(parts)),
        out_shape=(
            jax.ShapeDtypeStruct((block_rows, model), jnp.bfloat16),
            jax.ShapeDtypeStruct((block_rows, PAD), jnp.float32),
        ),
    )(*parts)
    handed = from_behind(grad_rows, "section", -1)
    return (gate_lanes[None, :, :routes], handed[None])


def solution(mesh):
    return jax.shard_map(
        body,
        mesh=mesh,
        in_specs=(
            P("section", "expert", None),
            P("section", "expert", None),
            P("section", None, None),
            P("section", None, None),
            P("section", "expert", None, None),
            P("section", "expert", None, None),
        ),
        out_specs=(P("section", "expert", None), P("section", "expert", None)),
        check_vma=False,
    )
```

```python
import functools

import jax
import jax.numpy as jnp
from jax import lax
from jax.experimental import pallas as pl
from jax.experimental.pallas import tpu as pltpu
from jax.sharding import PartitionSpec as P

PAD = 128


def slot_offsets(planes):
    half = planes // 2
    far = [(half + k, 0) for k in range(half)]
    near = [(k + 1, 0) for k in range(half - 1)] + [(0, 1)]
    slots = list(zip(far, near))
    return slots + [((a[0], 1), (b[0], 1 - b[1])) for a, b in slots]


def exchange(value, ahead, behind):
    pairs = []
    for here in range(lax.axis_size("expert")):
        z, y, c = here // 4, here // 2 % 2, here % 2
        dz, dy = ahead if c else behind
        pairs.append((here, (z ^ dz) * 4 + (y ^ dy) * 2 + c))
    return lax.ppermute(value, "expert", pairs)


def swap(value):
    return lax.ppermute(value, "expert", [(i, i ^ 1) for i in range(lax.axis_size("expert"))])


def from_behind(shard, axis, by):
    length = lax.axis_size(axis)
    pairs = [(i, i + by) for i in range(length) if 0 <= i + by < length]
    return lax.ppermute(shard, axis, pairs)


def after(value, *others):
    return lax.optimization_barrier((value,) + others)[0]


def in_hbm(value):
    return pltpu.with_memory_space_constraint(value, pltpu.HBM)


def pack_kernel(a_ref, b_ref, c_ref, d_ref, out_ref, sems):
    copies = [
        pltpu.make_async_copy(ref, out_ref.at[i], sems.at[i]) for i, ref in enumerate((a_ref, b_ref, c_ref, d_ref))
    ]
    for copy in copies:
        copy.start()
    for copy in copies:
        copy.wait()


def stage_kernel(planes, rows, ids_ref, gates_ref, up_ref, down_ref, _, out_ref, up_out, down_out, gate_ref, sems):
    copies = [
        pltpu.make_async_copy(up_ref, up_out, sems.at[0]),
        pltpu.make_async_copy(down_ref, down_out, sems.at[1]),
    ]
    for copy in copies:
        copy.start()
    position = lax.axis_index("expert")
    z, y, c = position // 4, position // 2 % 2, position % 2
    expert = position // (4 * planes // max(2, planes))
    match = (ids_ref[...] == expert).astype(jnp.float32)
    gate = jnp.sum(match * gates_ref[...].astype(jnp.float32), axis=0, keepdims=True)
    table = jnp.concatenate([gate, match, jnp.zeros((8 - 1 - match.shape[0], gate.shape[1]), jnp.float32)], axis=0)
    columns = jnp.transpose(table)
    gate_ref[...] = columns.reshape(gate_ref.shape)
    at = 0
    slots = slot_offsets(planes)
    for core in (c, c ^ 1):
        for ahead, behind in slots:
            dz = jnp.where(core == 1, ahead[0], behind[0])
            dy = jnp.where(core == 1, ahead[1], behind[1])
            chip = (z ^ dz) * 2 + (y ^ dy)
            for unit in (0, 1):
                out_ref[at:at + rows] = gate_ref[chip * 2 + (core ^ unit)]
                at += rows
    for copy in copies:
        copy.wait()


def grads_kernel(near, *refs):
    blocks, (chip_ref, aux_ref, gate_up_ref, down_ref, out_ref) = refs[:-5], refs[-5:]
    width = down_ref.shape[0]
    model = gate_up_ref.shape[1]
    units = [[ref[i] for i in range(4)] for ref in blocks]
    odd_core = lax.axis_index("expert") % 2 == 1
    chip = [chip_ref[i] for i in range(4)]
    if near:
        units[-1] = [jnp.where(odd_core, a, b) for a, b in zip(units[-1], chip)]
    else:
        units[-1] = [jnp.where(odd_core, b, a) for a, b in zip(units[-1], chip[2:] + chip[:2])]
    rows_in = jnp.concatenate([unit[i] for unit in units for i in (0, 2)], axis=0)
    rows_grad = jnp.concatenate([unit[i] for unit in units for i in (1, 3)], axis=0)
    contract = (((1,), (1,)), ((), ()))
    both = lax.dot_general(rows_in, gate_up_ref[...], contract, preferred_element_type=jnp.float32)
    back = lax.dot_general(rows_grad, down_ref[...], contract, preferred_element_type=jnp.float32)
    first = both[:, :width]
    second = both[:, width:]
    sigma = jax.nn.sigmoid(first)
    active = first * sigma
    gate = aux_ref[:, 0:1]
    slot_grad = jnp.sum(back * active * second, axis=1, keepdims=True)
    scaled = gate * back
    d_first = scaled * second * sigma * (1.0 + first * (1.0 - sigma))
    d_second = scaled * active
    d_both = jnp.concatenate([d_first, d_second], axis=1).astype(jnp.bfloat16)
    contrib = jnp.dot(d_both, gate_up_ref[...], preferred_element_type=jnp.float32)
    out_ref[:, :model] = contrib.astype(out_ref.dtype)
    lane = lax.broadcasted_iota(jnp.int32, (slot_grad.shape[0], PAD), 1)
    picked = jnp.where(lane % 2 == 0, aux_ref[:, 1:2], aux_ref[:, 2:3]) * slot_grad
    high = picked.astype(jnp.bfloat16).astype(jnp.float32)
    place = lane - (0 if near else 4)
    packed = jnp.where(place // 2 == 0, high, jnp.where(place // 2 == 1, picked - high, 0.0))
    out_ref[:, model:] = packed.astype(out_ref.dtype)


def expert_grads(near, blocks, chip, aux, gate_up, down_mat):
    rows = aux.shape[0]
    model = gate_up.shape[1]
    return pl.pallas_call(
        functools.partial(grads_kernel, near),
        out_shape=jax.ShapeDtypeStruct((rows, model + PAD), jnp.float32 if near else jnp.bfloat16),
        compiler_params=pltpu.CompilerParams(vmem_limit_bytes=16 << 20),
        cost_estimate=pl.CostEstimate(
            flops=2 * rows * model * (2 * gate_up.shape[0] + down_mat.shape[0]),
            transcendentals=rows * down_mat.shape[0],
            bytes_accessed=2 * model * (2 * rows + gate_up.shape[0] + down_mat.shape[0]),
        ),
    )(*blocks, chip, aux, gate_up, down_mat)


def body(tokens, out_grad, expert_ids, gate_weights, gate_up_rows, down_rows):
    size = lax.axis_size("expert")
    planes = size // 4
    half = planes // 2
    rows = tokens.shape[1]
    model = tokens.shape[2]
    routes = expert_ids.shape[2]
    gate_up = gate_up_rows[0, 0]
    down_mat = down_rows[0, 0]
    slots = slot_offsets(planes)

    other_in = swap(tokens[0])
    other_grad = swap(out_grad[0])
    anywhere = pl.BlockSpec(memory_space=pl.ANY)
    chip = pl.pallas_call(
        pack_kernel,
        in_specs=[anywhere] * 2 + [pl.BlockSpec(memory_space=pltpu.VMEM)] * 2,
        out_specs=anywhere,
        out_shape=jax.ShapeDtypeStruct((4,) + tokens.shape[1:], tokens.dtype),
        scratch_shapes=[pltpu.SemaphoreType.DMA((4,))],
        compiler_params=pltpu.CompilerParams(vmem_limit_bytes=1 << 20),
    )(in_hbm(tokens[0]), in_hbm(out_grad[0]), other_in, other_grad)
    held = pl.BlockSpec(memory_space=pltpu.VMEM)
    aux, gate_up, down_mat = pl.pallas_call(
        functools.partial(stage_kernel, planes, rows),
        in_specs=[held] * 2 + [anywhere] * 3,
        out_specs=[held] * 3,
        out_shape=(
            jax.ShapeDtypeStruct((size * rows, 8), jnp.float32),
            jax.ShapeDtypeStruct(gate_up.shape, gate_up.dtype),
            jax.ShapeDtypeStruct(down_mat.shape, down_mat.dtype),
        ),
        scratch_shapes=[pltpu.VMEM((size, rows, 8), jnp.float32), pltpu.SemaphoreType.DMA((2,))],
        compiler_params=pltpu.CompilerParams(vmem_limit_bytes=8 << 20),
        cost_estimate=pl.CostEstimate(
            flops=0, transcendentals=0, bytes_accessed=4 * model * (gate_up.shape[0] + down_mat.shape[0])
        ),
    )(expert_ids[0].T, gate_weights[0].T, in_hbm(gate_up), in_hbm(down_mat), chip)

    direct = [exchange(chip, *slots[k]) for k in range(half)]
    direct[0] = after(direct[0], aux)
    for k in range(half):
        direct.append(exchange(direct[k], (0, 1), (0, 1) if k < half - 1 else (0, 0)))
    gate = direct[-2]
    swapped = [swap(after(value, gate)) for value in direct[:half]] + [swap(value) for value in direct[half:]]
    near = size * rows // 2
    send = expert_grads(False, swapped, chip, aux[near:], gate_up, down_mat)
    keep = expert_grads(True, direct, chip, aux[:near], gate_up, down_mat)
    total = (keep + swap(send).astype(jnp.float32)).astype(jnp.bfloat16)
    received = [exchange(total[k * 2 * rows:(k + 1) * 2 * rows], *slots[k]) for k in range(planes)]
    total = sum(part.astype(jnp.float32) for part in received)
    final = total[:rows] + swap(total[rows:])
    grad_rows = final[:, :model].astype(jnp.bfloat16)
    lanes = final[:, model:model + 8].reshape(rows, 4, routes)
    gate_grad = jnp.sum(lanes, axis=1)
    handed = from_behind(grad_rows, "section", -1)
    return (gate_grad[None], handed[None])


def solution(mesh):
    return jax.shard_map(
        body,
        mesh=mesh,
        in_specs=(
            P("section", "expert", None),
            P("section", "expert", None),
            P("section", None, None),
            P("section", None, None),
            P("section", "expert", None, None),
            P("section", "expert", None, None),
        ),
        out_specs=(P("section", "expert", None), P("section", "expert", None)),
        check_vma=False,
    )
```

```python
import functools

import jax
import jax.numpy as jnp
from jax import lax
from jax.experimental import pallas as pl
from jax.experimental.pallas import tpu as pltpu
from jax.sharding import PartitionSpec as P

PAD = 128


def slot_offsets(planes):
    half = planes // 2
    far = [(half + k, 0) for k in range(half)]
    near = [(k + 1, 0) for k in range(half - 1)] + [(0, 1)]
    slots = list(zip(far, near))
    return slots + [((a[0], 1), (b[0], 1 - b[1])) for a, b in slots]


def exchange(value, ahead, behind):
    pairs = []
    for here in range(lax.axis_size("expert")):
        z, y, c = here // 4, here // 2 % 2, here % 2
        dz, dy = ahead if c else behind
        pairs.append((here, (z ^ dz) * 4 + (y ^ dy) * 2 + c))
    return lax.ppermute(value, "expert", pairs)


def swap(value):
    return lax.ppermute(value, "expert", [(i, i ^ 1) for i in range(lax.axis_size("expert"))])


def from_behind(shard, axis, by):
    length = lax.axis_size(axis)
    pairs = [(i, i + by) for i in range(length) if 0 <= i + by < length]
    return lax.ppermute(shard, axis, pairs)


def after(value, *others):
    return lax.optimization_barrier((value,) + others)[0]


def in_hbm(value):
    return pltpu.with_memory_space_constraint(value, pltpu.HBM)


def load_kernel(a_ref, b_ref, out_ref, sems):
    copies = [pltpu.make_async_copy(ref, out_ref.at[i], sems.at[i]) for i, ref in enumerate((a_ref, b_ref))]
    for copy in copies:
        copy.start()
    for copy in copies:
        copy.wait()


def pack_kernel(own_ref, a_ref, b_ref, out_ref):
    out_ref[0:2] = own_ref[...]
    out_ref[2] = a_ref[...]
    out_ref[3] = b_ref[...]


def stage_kernel(planes, rows, ids_ref, gates_ref, up_ref, down_ref, _, out_ref, up_out, up_flip, down_flip, gate_ref, down_out, sems):
    copies = [
        pltpu.make_async_copy(up_ref, up_out, sems.at[0]),
        pltpu.make_async_copy(down_ref, down_out, sems.at[1]),
    ]
    for copy in copies:
        copy.start()
    position = lax.axis_index("expert")
    z, y, c = position // 4, position // 2 % 2, position % 2
    expert = position // (4 * planes // max(2, planes))
    match = (ids_ref[...] == expert).astype(jnp.float32)
    gate = jnp.sum(match * gates_ref[...].astype(jnp.float32), axis=0, keepdims=True)
    table = jnp.concatenate([gate, match, jnp.zeros((8 - 1 - match.shape[0], gate.shape[1]), jnp.float32)], axis=0)
    columns = jnp.transpose(table)
    gate_ref[...] = columns.reshape(gate_ref.shape)
    at = 0
    half = planes // 2
    slots = slot_offsets(planes)
    for core, group in ((c, slots[:half]), (c ^ 1, slots[:half]), (c, slots[half:]), (c ^ 1, slots[half:])):
        for ahead, behind in group:
            dz = jnp.where(core == 1, ahead[0], behind[0])
            dy = jnp.where(core == 1, ahead[1], behind[1])
            chip = (z ^ dz) * 2 + (y ^ dy)
            for unit in (0, 1):
                out_ref[at:at + rows] = gate_ref[chip * 2 + (core ^ unit)]
                at += rows
    for copy in copies:
        copy.wait()
    up_flip[...] = jnp.transpose(up_out[...])
    down_flip[...] = jnp.transpose(down_out[...])


def grads_kernel(count, own, *refs):
    blocks, (aux_ref, gate_up_ref, up_flip_ref, down_flip_ref, keep_ref, send_ref) = refs[:count], refs[-6:]
    width = down_flip_ref.shape[1]
    model = gate_up_ref.shape[1]
    near = keep_ref.shape[0]
    units = [[ref[i] for i in range(4)] for ref in blocks]
    if own:
        odd_core = lax.axis_index("expert") % 2 == 1
        chip = [refs[count][i] for i in range(4)]
        units[count // 2 - 1] = [jnp.where(odd_core, a, b) for a, b in zip(units[count // 2 - 1], chip)]
        units[-1] = [jnp.where(odd_core, b, a) for a, b in zip(units[-1], chip[2:] + chip[:2])]
    rows_in = jnp.concatenate([unit[i] for unit in units for i in (0, 2)], axis=0)
    rows_grad = jnp.concatenate([unit[i] for unit in units for i in (1, 3)], axis=0)
    both = jnp.dot(rows_in, up_flip_ref[...], preferred_element_type=jnp.float32)
    back = jnp.dot(rows_grad, down_flip_ref[...], preferred_element_type=jnp.float32)
    first = both[:, :width]
    second = both[:, width:]
    sigma = jax.nn.sigmoid(first)
    active = first * sigma
    gate = aux_ref[:, 0:1]
    slot_grad = jnp.sum(back * active * second, axis=1, keepdims=True)
    scaled = gate * back
    d_first = scaled * second * sigma * (1.0 + first * (1.0 - sigma))
    d_second = scaled * active
    d_both = jnp.concatenate([d_first, d_second], axis=1).astype(jnp.bfloat16)
    contrib = jnp.dot(d_both, gate_up_ref[...], preferred_element_type=jnp.float32)
    keep_ref[:, :model] = contrib[:near]
    send_ref[:, :model] = contrib[near:].astype(jnp.bfloat16)
    rows = slot_grad.shape[0]
    lane = lax.broadcasted_iota(jnp.int32, (rows, PAD), 1)
    row = lax.broadcasted_iota(jnp.int32, (rows, PAD), 0)
    picked = jnp.where(lane % 2 == 0, aux_ref[:, 1:2], aux_ref[:, 2:3]) * slot_grad
    high = picked.astype(jnp.bfloat16).astype(jnp.float32)
    place = lane - jnp.where(row < near, 0, 4)
    packed = jnp.where(place // 2 == 0, high, jnp.where(place // 2 == 1, picked - high, 0.0))
    keep_ref[:, model:] = packed[:near]
    send_ref[:, model:] = packed[near:].astype(jnp.bfloat16)


def expert_grads(blocks, own, aux, weights):
    rows = aux.shape[0]
    width, model = weights[0].shape
    return pl.pallas_call(
        functools.partial(grads_kernel, len(blocks), bool(own)),
        out_shape=(
            jax.ShapeDtypeStruct((rows // 2, model + PAD), jnp.float32),
            jax.ShapeDtypeStruct((rows // 2, model + PAD), jnp.bfloat16),
        ),
        compiler_params=pltpu.CompilerParams(vmem_limit_bytes=16 << 20),
        cost_estimate=pl.CostEstimate(
            flops=5 * rows * model * width,
            transcendentals=rows * width // 2,
            bytes_accessed=2 * model * (2 * rows) + 3 * model * width,
        ),
    )(*blocks, *own, aux, *weights)


def body(tokens, out_grad, expert_ids, gate_weights, gate_up_rows, down_rows):
    size = lax.axis_size("expert")
    planes = size // 4
    half = planes // 2
    rows = tokens.shape[1]
    model = tokens.shape[2]
    routes = expert_ids.shape[2]
    gate_up = gate_up_rows[0, 0]
    down_mat = down_rows[0, 0]
    slots = slot_offsets(planes)

    other_in = swap(tokens[0])
    other_grad = swap(out_grad[0])
    anywhere = pl.BlockSpec(memory_space=pl.ANY)
    held = pl.BlockSpec(memory_space=pltpu.VMEM)
    own = pl.pallas_call(
        load_kernel,
        in_specs=[anywhere] * 2,
        out_specs=held,
        out_shape=jax.ShapeDtypeStruct((2,) + tokens.shape[1:], tokens.dtype),
        scratch_shapes=[pltpu.SemaphoreType.DMA((2,))],
        compiler_params=pltpu.CompilerParams(vmem_limit_bytes=1 << 20),
    )(in_hbm(tokens[0]), in_hbm(out_grad[0]))
    chip = pl.pallas_call(
        pack_kernel,
        in_specs=[held] * 3,
        out_specs=held,
        out_shape=jax.ShapeDtypeStruct((4,) + tokens.shape[1:], tokens.dtype),
        compiler_params=pltpu.CompilerParams(vmem_limit_bytes=1 << 20),
    )(own, other_in, other_grad)
    aux, *weights = pl.pallas_call(
        functools.partial(stage_kernel, planes, rows),
        in_specs=[held] * 2 + [anywhere] * 3,
        out_specs=[held] * 4,
        out_shape=(
            jax.ShapeDtypeStruct((size * rows, 8), jnp.float32),
            jax.ShapeDtypeStruct(gate_up.shape, gate_up.dtype),
            jax.ShapeDtypeStruct(gate_up.shape[::-1], gate_up.dtype),
            jax.ShapeDtypeStruct(down_mat.shape[::-1], down_mat.dtype),
        ),
        scratch_shapes=[
            pltpu.VMEM((size, rows, 8), jnp.float32),
            pltpu.VMEM(down_mat.shape, down_mat.dtype),
            pltpu.SemaphoreType.DMA((2,)),
        ],
        compiler_params=pltpu.CompilerParams(vmem_limit_bytes=16 << 20),
        cost_estimate=pl.CostEstimate(
            flops=0, transcendentals=0, bytes_accessed=4 * model * (gate_up.shape[0] + down_mat.shape[0])
        ),
    )(expert_ids[0].T, gate_weights[0].T, in_hbm(gate_up), in_hbm(down_mat), chip)

    first = [exchange(chip, *slots[k]) for k in range(half)]
    first[0] = after(first[0], aux)
    then = [exchange(first[k], (0, 1), (0, 1) if k < half - 1 else (0, 0)) for k in range(half)]
    swapped = [swap(after(value, first[-1])) for value in first[:-1]] + [swap(after(first[-1], then[0]))]
    near = size * rows // 2
    keep, send1 = expert_grads(first + swapped, [], aux[:near], weights)
    came = after(swap(send1), then[-1])
    total1 = (keep + came.astype(jnp.float32)).astype(jnp.bfloat16)
    late = [value for value in then[:-1]]
    late.append(then[-1])
    swapped = [swap(value) for value in late]
    keep, send = expert_grads(late + swapped, [chip], aux[near:], weights)
    total = (keep + swap(send).astype(jnp.float32)).astype(jnp.bfloat16)
    received = [exchange(total1[k * 2 * rows:(k + 1) * 2 * rows], *slots[k]) for k in range(half)]
    received += [exchange(total[k * 2 * rows:(k + 1) * 2 * rows], *slots[half + k]) for k in range(half)]
    total = sum(part.astype(jnp.float32) for part in received)
    final = total[:rows] + swap(total[rows:])
    grad_rows = final[:, :model].astype(jnp.bfloat16)
    lanes = final[:, model:model + 8].reshape(rows, 4, routes)
    gate_grad = jnp.sum(lanes, axis=1)
    handed = from_behind(grad_rows, "section", -1)
    return (gate_grad[None], handed[None])


def solution(mesh):
    return jax.shard_map(
        body,
        mesh=mesh,
        in_specs=(
            P("section", "expert", None),
            P("section", "expert", None),
            P("section", None, None),
            P("section", None, None),
            P("section", "expert", None, None),
            P("section", "expert", None, None),
        ),
        out_specs=(P("section", "expert", None), P("section", "expert", None)),
        check_vma=False,
    )
```

```python
import functools

import jax
import jax.numpy as jnp
from jax import lax
from jax.experimental import pallas as pl
from jax.experimental.pallas import tpu as pltpu
from jax.sharding import PartitionSpec as P

PAD = 128


def slot_offsets(planes):
    half = planes // 2
    far = [(half + k, 0) for k in range(half)]
    near = [(k + 1, 0) for k in range(half - 1)] + [(0, 1)]
    slots = list(zip(far, near))
    return slots + [((a[0], 1), (b[0], 1 - b[1])) for a, b in slots]


def exchange(value, ahead, behind):
    pairs = []
    for here in range(lax.axis_size("expert")):
        z, y, c = here // 4, here // 2 % 2, here % 2
        dz, dy = ahead if c else behind
        pairs.append((here, (z ^ dz) * 4 + (y ^ dy) * 2 + c))
    return lax.ppermute(value, "expert", pairs)


def swap(value):
    return lax.ppermute(value, "expert", [(i, i ^ 1) for i in range(lax.axis_size("expert"))])


def from_behind(shard, axis, by):
    length = lax.axis_size(axis)
    pairs = [(i, i + by) for i in range(length) if 0 <= i + by < length]
    return lax.ppermute(shard, axis, pairs)


def after(value, *others):
    return lax.optimization_barrier((value,) + others)[0]


def in_hbm(value):
    return pltpu.with_memory_space_constraint(value, pltpu.HBM)


def load_kernel(a_ref, b_ref, out_ref, sems):
    copies = [pltpu.make_async_copy(ref, out_ref.at[i], sems.at[i]) for i, ref in enumerate((a_ref, b_ref))]
    for copy in copies:
        copy.start()
    for copy in copies:
        copy.wait()


def pack_kernel(own_ref, a_ref, b_ref, out_ref):
    out_ref[0:2] = own_ref[...]
    out_ref[2] = a_ref[...]
    out_ref[3] = b_ref[...]


def stage_kernel(planes, rows, ids_ref, gates_ref, up_ref, down_ref, _, out_ref, up_out, up_flip, down_flip, gate_ref, down_out, sems):
    copies = [
        pltpu.make_async_copy(up_ref, up_out, sems.at[0]),
        pltpu.make_async_copy(down_ref, down_out, sems.at[1]),
    ]
    for copy in copies:
        copy.start()
    position = lax.axis_index("expert")
    z, y, c = position // 4, position // 2 % 2, position % 2
    expert = position // (4 * planes // max(2, planes))
    match = (ids_ref[...] == expert).astype(jnp.float32)
    gate = jnp.sum(match * gates_ref[...].astype(jnp.float32), axis=0, keepdims=True)
    table = jnp.concatenate([gate, match, jnp.zeros((8 - 1 - match.shape[0], gate.shape[1]), jnp.float32)], axis=0)
    columns = jnp.transpose(table)
    gate_ref[...] = columns.reshape(gate_ref.shape)
    at = 0
    half = planes // 2
    slots = slot_offsets(planes)
    for core, group in ((c, slots[:half]), (c ^ 1, slots[:half]), (c, slots[half:]), (c ^ 1, slots[half:])):
        for ahead, behind in group:
            dz = jnp.where(core == 1, ahead[0], behind[0])
            dy = jnp.where(core == 1, ahead[1], behind[1])
            chip = (z ^ dz) * 2 + (y ^ dy)
            for unit in (0, 1):
                out_ref[at:at + rows] = gate_ref[chip * 2 + (core ^ unit)]
                at += rows
    for copy in copies:
        copy.wait()
    up_flip[...] = jnp.transpose(up_out[...])
    down_flip[...] = jnp.transpose(down_out[...])


def grads_kernel(count, own, *refs):
    blocks, (aux_ref, gate_up_ref, up_flip_ref, down_flip_ref, keep_ref, send_ref) = refs[:count], refs[-6:]
    width = down_flip_ref.shape[1]
    model = gate_up_ref.shape[1]
    near = keep_ref.shape[0]
    units = [[ref[i] for i in range(4)] for ref in blocks]
    if own:
        odd_core = lax.axis_index("expert") % 2 == 1
        chip = [refs[count][i] for i in range(4)]
        units[count // 2 - 1] = [jnp.where(odd_core, a, b) for a, b in zip(units[count // 2 - 1], chip)]
        units[-1] = [jnp.where(odd_core, b, a) for a, b in zip(units[-1], chip[2:] + chip[:2])]
    rows_in = jnp.concatenate([unit[i] for unit in units for i in (0, 2)], axis=0)
    rows_grad = jnp.concatenate([unit[i] for unit in units for i in (1, 3)], axis=0)
    both = jnp.dot(rows_in, up_flip_ref[...], preferred_element_type=jnp.float32)
    back = jnp.dot(rows_grad, down_flip_ref[...], preferred_element_type=jnp.float32)
    first = both[:, :width]
    second = both[:, width:]
    sigma = jax.nn.sigmoid(first)
    active = first * sigma
    gate = aux_ref[:, 0:1]
    slot_grad = jnp.sum(back * active * second, axis=1, keepdims=True)
    scaled = gate * back
    d_first = scaled * second * sigma * (1.0 + first * (1.0 - sigma))
    d_second = scaled * active
    d_both = jnp.concatenate([d_first, d_second], axis=1).astype(jnp.bfloat16)
    contrib = jnp.dot(d_both, gate_up_ref[...], preferred_element_type=jnp.float32)
    keep_ref[:, :model] = contrib[:near]
    send_ref[:, :model] = contrib[near:].astype(jnp.bfloat16)
    rows = slot_grad.shape[0]
    lane = lax.broadcasted_iota(jnp.int32, (rows, PAD), 1)
    row = lax.broadcasted_iota(jnp.int32, (rows, PAD), 0)
    picked = jnp.where(lane % 2 == 0, aux_ref[:, 1:2], aux_ref[:, 2:3]) * slot_grad
    high = picked.astype(jnp.bfloat16).astype(jnp.float32)
    place = lane - jnp.where(row < near, 0, 4)
    packed = jnp.where(place // 2 == 0, high, jnp.where(place // 2 == 1, picked - high, 0.0))
    keep_ref[:, model:] = packed[:near]
    send_ref[:, model:] = packed[near:].astype(jnp.bfloat16)


def expert_grads(blocks, own, aux, weights):
    rows = aux.shape[0]
    width, model = weights[0].shape
    return pl.pallas_call(
        functools.partial(grads_kernel, len(blocks), bool(own)),
        out_shape=(
            jax.ShapeDtypeStruct((rows // 2, model + PAD), jnp.float32),
            jax.ShapeDtypeStruct((rows // 2, model + PAD), jnp.bfloat16),
        ),
        compiler_params=pltpu.CompilerParams(vmem_limit_bytes=16 << 20),
        cost_estimate=pl.CostEstimate(
            flops=5 * rows * model * width,
            transcendentals=rows * width // 2,
            bytes_accessed=2 * model * (2 * rows) + 3 * model * width,
        ),
    )(*blocks, *own, aux, *weights)


def body(tokens, out_grad, expert_ids, gate_weights, gate_up_rows, down_rows):
    size = lax.axis_size("expert")
    planes = size // 4
    half = planes // 2
    rows = tokens.shape[1]
    model = tokens.shape[2]
    routes = expert_ids.shape[2]
    gate_up = gate_up_rows[0, 0]
    down_mat = down_rows[0, 0]
    slots = slot_offsets(planes)

    other_in = swap(tokens[0])
    other_grad = swap(out_grad[0])
    anywhere = pl.BlockSpec(memory_space=pl.ANY)
    held = pl.BlockSpec(memory_space=pltpu.VMEM)
    own = pl.pallas_call(
        load_kernel,
        in_specs=[anywhere] * 2,
        out_specs=held,
        out_shape=jax.ShapeDtypeStruct((2,) + tokens.shape[1:], tokens.dtype),
        scratch_shapes=[pltpu.SemaphoreType.DMA((2,))],
        compiler_params=pltpu.CompilerParams(vmem_limit_bytes=1 << 20),
    )(in_hbm(tokens[0]), in_hbm(out_grad[0]))
    chip = pl.pallas_call(
        pack_kernel,
        in_specs=[held] * 3,
        out_specs=held,
        out_shape=jax.ShapeDtypeStruct((4,) + tokens.shape[1:], tokens.dtype),
        compiler_params=pltpu.CompilerParams(vmem_limit_bytes=1 << 20),
    )(own, other_in, other_grad)
    aux, *weights = pl.pallas_call(
        functools.partial(stage_kernel, planes, rows),
        in_specs=[held] * 2 + [anywhere] * 3,
        out_specs=[held] * 4,
        out_shape=(
            jax.ShapeDtypeStruct((size * rows, 8), jnp.float32),
            jax.ShapeDtypeStruct(gate_up.shape, gate_up.dtype),
            jax.ShapeDtypeStruct(gate_up.shape[::-1], gate_up.dtype),
            jax.ShapeDtypeStruct(down_mat.shape[::-1], down_mat.dtype),
        ),
        scratch_shapes=[
            pltpu.VMEM((size, rows, 8), jnp.float32),
            pltpu.VMEM(down_mat.shape, down_mat.dtype),
            pltpu.SemaphoreType.DMA((2,)),
        ],
        compiler_params=pltpu.CompilerParams(vmem_limit_bytes=16 << 20),
        cost_estimate=pl.CostEstimate(
            flops=0, transcendentals=0, bytes_accessed=4 * model * (gate_up.shape[0] + down_mat.shape[0])
        ),
    )(expert_ids[0].T, gate_weights[0].T, in_hbm(gate_up), in_hbm(down_mat), chip)

    first = [exchange(chip, *slots[k]) for k in range(half)]
    first[-1] = after(first[-1], aux)
    then = [exchange(first[k], (0, 1), (0, 1) if k < half - 1 else (0, 0)) for k in range(half)]
    swapped = [swap(after(value, first[-1])) for value in first[:-1]] + [swap(first[-1])]
    near = size * rows // 2
    keep, send1 = expert_grads(first + swapped, [], after(aux[:near], then[0]), weights)
    came = after(swap(send1), then[-1])
    total1 = (keep + came.astype(jnp.float32)).astype(jnp.bfloat16)
    received = [exchange(total1[k * 2 * rows:(k + 1) * 2 * rows], *slots[k]) for k in range(half)]
    swapped = [swap(value) for value in then]
    keep, send = expert_grads(then + swapped, [chip], aux[near:], weights)
    came = after(swap(send), total1)
    total = (keep + came.astype(jnp.float32)).astype(jnp.bfloat16)
    received += [exchange(total[k * 2 * rows:(k + 1) * 2 * rows], *slots[half + k]) for k in range(half)]
    total = sum(part.astype(jnp.float32) for part in received)
    final = total[:rows] + swap(total[rows:])
    grad_rows = final[:, :model].astype(jnp.bfloat16)
    lanes = final[:, model:model + 8].reshape(rows, 4, routes)
    gate_grad = jnp.sum(lanes, axis=1)
    handed = from_behind(grad_rows, "section", -1)
    return (gate_grad[None], handed[None])


def solution(mesh):
    return jax.shard_map(
        body,
        mesh=mesh,
        in_specs=(
            P("section", "expert", None),
            P("section", "expert", None),
            P("section", None, None),
            P("section", None, None),
            P("section", "expert", None, None),
            P("section", "expert", None, None),
        ),
        out_specs=(P("section", "expert", None), P("section", "expert", None)),
        check_vma=False,
    )
```
